32 devices in a mesh: obs: 16 (over z, x, core), cell: 2 (over y).
Axes of the slice: x: 2, y: 2, z: 4, core: 2. Of those that a mesh axis runs over, the one named last changes fastest.
Arguments:
- flux_field: bfloat16 [2, 16, 64, 128], P('cell', 'obs'), may hold values from -6 to 6
- footprint: bfloat16 [256, 16, 128, 128], P('obs', 'cell'), may hold values from -0.125 to 0.125
- block_index: int32 [256, 16], P('obs', 'cell'), may hold values from 0 to 15
- tile_count: int32 [16], P('obs'), may hold values from 1 to 16, 128 in all
- sounding_week: int32 [256, 128], P('obs'), may hold values from 0 to 3
- member_ids: int32 [16], replicated, may hold values from 0 to 15, each once
- observed: float32 [256, 128], P('obs'), may hold values from -6 to 6
- perturb: bfloat16 [256, 16, 128], P('obs'), may hold values from -6 to 6
- obs_weight: float32 [256, 128], P('obs'), may hold values from 0.3 to 3
Outputs:
- gradient: float32 [2, 16, 64, 128], P('cell', 'obs')
- residual: bfloat16 [256, 16, 128], P('obs')
The draws below stay inside these ranges and needn't reach their ends.
All inputs are finite; a program needn't handle non-finite values. No bound on the sum of `tile_count` on one device may be relied on, other than what follows from the above.
Results may differ from the reference program's by a relative error of at most 0.0028.
Values may be sent and summed in bfloat16 or wider, within the bound.
No kernel may reach another device: no remote copies, remote signals or barrier semaphores. Data moves between devices by JAX's collectives and lax.ppermute only.
A program may use at most 64 MiB of HBM per device.

```python
import math
import jax
import jax.numpy as jnp
import numpy as np
from jax import lax

MEMBERS = 16
WEEKS = 4
BLOCK_CELLS = 128
TILE_SOUNDINGS = 128
TILE_BLOCKS = 8
TILE_SLOTS = 16
SLABS = 2
SLAB_BLOCKS = 16
TILES = 256
N_OBS = 16


def touch_ends(entries, stream_key, smallest, top_value):
    longest = entries.shape.index(max(entries.shape))
    spots = []
    for shift in (0, 1):
        where = [jax.random.randint(jax.random.fold_in(stream_key, axis), (), 0, length) for axis, length in enumerate(entries.shape)]
        where[longest] = (where[longest] + shift) % entries.shape[longest]
        spots.append(tuple(where))
    return entries.at[spots[0]].set(smallest).at[spots[1]].set(top_value)


def block_levels(key, shape, cuts, least, high):
    level, own = 1.0, jax.random.fold_in(key, 6)
    for dim, shards_of in cuts:
        steps = jnp.exp(jax.random.uniform(jax.random.fold_in(own, dim), (shards_of,), jnp.float32, least / len(cuts), high / len(cuts)))
        level = level * jnp.repeat(steps, shape[dim] // shards_of).reshape([-1 if axis == dim else 1 for axis in range(len(shape))])
    return level


def length_profile(number_of, total, bound, skew):
    loads = [(1 << 20) // math.isqrt(grade ** skew) + 1 for grade in range(2, number_of + 1)]
    surplus, holding = total - bound - (number_of - 1), [1] * (number_of - 1)
    while surplus > 0:
        candidates = [i for i in range(number_of - 1) if holding[i] < bound]
        pool, left = sum([loads[i] for i in candidates]), surplus
        for i in candidates:
            more = min(bound - holding[i], max(1, left * loads[i] // pool), surplus)
            holding[i] = holding[i] + more
            surplus = surplus - more
    return np.array([bound] + holding)


def ragged_sizes(key, number_of, total, bound, lean):
    if number_of == 2:
        one = jax.random.randint(key, (), max(1, total - bound), min(bound, total - 1) + 1)
        return jnp.stack([one, total - one])
    lengths = jnp.asarray(length_profile(number_of, total, bound, lean), jnp.int32)
    twos = (number_of - 1) // 2
    source_of, sink = lengths[1:1 + 2 * twos:2], lengths[2:2 + 2 * twos:2]
    margin = jnp.minimum(source_of - 1, bound - sink)
    passed = jax.random.randint(jax.random.fold_in(key, 1), (twos,), 0, 1 << 20) % (margin + 1)
    lengths = lengths.at[1:1 + 2 * twos:2].set(source_of - passed).at[2:2 + 2 * twos:2].set(sink + passed)
    return lengths[jax.random.permutation(jax.random.fold_in(key, 2), number_of)]


def centred(key, dims, width, most, shards=(), kind=jnp.bfloat16):
    drawn = width * jax.random.normal(key, dims, jnp.float32)
    if shards:
        drawn = drawn * block_levels(key, dims, shards, -0.22, 0.18)
    return jnp.clip(drawn, -most, most).astype(kind)


def setup_inputs(seed: int = 0) -> dict:
    splits = jax.random.split(jax.random.key(seed), 10)
    flux_field = centred(splits[0], (SLABS, SLAB_BLOCKS, WEEKS * MEMBERS, BLOCK_CELLS), 1.0, 6.0, ((0, 2), (1, 16)))
    footprint = centred(splits[1], (TILES, SLABS * TILE_BLOCKS, TILE_SOUNDINGS, BLOCK_CELLS), (SLABS * TILE_BLOCKS * BLOCK_CELLS) ** -0.5, 0.125, ((0, 16), (1, 2)))
    block_index = touch_ends(jax.random.randint(splits[2], (TILES, SLABS * TILE_BLOCKS), 0, SLAB_BLOCKS), jax.random.fold_in(splits[2], 1), 0, SLAB_BLOCKS - 1).astype(jnp.int32)
    tile_count = ragged_sizes(splits[3], N_OBS, N_OBS * TILE_SLOTS // 2, TILE_SLOTS, 2).astype(jnp.int32)
    sounding_week = touch_ends(jax.random.randint(splits[4], (TILES, TILE_SOUNDINGS), 0, WEEKS), jax.random.fold_in(splits[4], 1), 0, WEEKS - 1).astype(jnp.int32)
    member_ids = jax.random.permutation(splits[5], MEMBERS).astype(jnp.int32)
    observed = centred(splits[6], (TILES, TILE_SOUNDINGS), 1.0, 6.0, ((0, 16),), jnp.float32)
    perturb = centred(splits[7], (TILES, MEMBERS, TILE_SOUNDINGS), 1.0, 6.0, ((0, 16),))
    obs_weight = jnp.clip(jnp.exp(math.log(3.0) - 2.3025851 * jax.random.uniform(splits[8], (TILES, TILE_SOUNDINGS), jnp.float32) ** block_levels(splits[8], (TILES, TILE_SOUNDINGS), ((0, 16),), -0.2, 0.2)), 0.3, 3.0)
    return dict(flux_field=flux_field, footprint=footprint, block_index=block_index, tile_count=tile_count, sounding_week=sounding_week, member_ids=member_ids, observed=observed, perturb=perturb, obs_weight=obs_weight)


def reference(flux_field, footprint, block_index, tile_count, sounding_week, member_ids, observed, perturb, obs_weight):
    rows_all = WEEKS * MEMBERS
    slab_of = (jnp.arange(SLABS * TILE_BLOCKS) // TILE_BLOCKS).astype(jnp.int32)
    week_ids = jnp.arange(WEEKS).astype(jnp.int32)

    def one_tile(carry, inputs):
        tile_no, sens, blocks, weeks_of, seen, noise, weights = inputs
        alive = (tile_no % TILE_SLOTS < tile_count[tile_no // TILE_SLOTS]).astype(jnp.float32)
        chosen = flux_field[slab_of, blocks].astype(jnp.float32)
        mixing = jnp.einsum('jrc,jsc->rs', chosen, sens.astype(jnp.float32))
        week_hot = (weeks_of[None, :] == week_ids[:, None]).astype(jnp.float32)
        modeled = jnp.einsum('wms,ws->ms', mixing.reshape(WEEKS, MEMBERS, -1), week_hot)
        shifted = noise[member_ids].astype(jnp.float32)
        residual = (alive * weights[None, :] * (modeled - seen[None, :] - shifted)).astype(jnp.bfloat16)
        adjoint_rows = (residual.astype(jnp.float32)[None] * week_hot[:, None, :]).reshape(rows_all, -1)
        contrib = jnp.einsum('rs,jsc->jrc', adjoint_rows, sens.astype(jnp.float32))
        carry = carry.at[slab_of, blocks].add(contrib)
        return carry, residual

    start = jnp.zeros((SLABS, SLAB_BLOCKS, rows_all, BLOCK_CELLS), jnp.float32)
    tiles_no = jnp.arange(TILES).astype(jnp.int32)
    gradient, residual = lax.scan(one_tile, start, (tiles_no, footprint, block_index, sounding_week, observed, perturb, obs_weight))
    return gradient, residual
```

```python
import functools

import jax
import jax.numpy as jnp
from jax import lax
from jax.experimental import pallas as pl
from jax.experimental.pallas import tpu as pltpu
from jax.sharding import PartitionSpec as P

MEMBERS = 16
WEEKS = 4
ROWS = WEEKS * MEMBERS

VMEM = pl.BlockSpec(memory_space=pltpu.VMEM)
SMEM = pl.BlockSpec(memory_space=pltpu.SMEM)


def phases_of(count):
    bits = [1 << i for i in range(count.bit_length() - 1)]
    upper = bits[:0:-1]
    rounds = [upper[:1]] if len(upper) % 2 else []
    rest = upper[len(upper) % 2 :]
    rounds += [rest[i : i + 2] for i in range(0, len(rest), 2)]
    return rounds + [bits[:1]]


def masks_of(bits):
    masks = [0]
    for bit in bits:
        masks += [mask | bit for mask in masks]
    return masks


def order_of(rounds):
    order = [0]
    for bits in rounds:
        order = [mask | low for mask in masks_of(bits) for low in order]
    return order


def swap(value, axis, count, mask):
    return lax.ppermute(value, axis, [(i, i ^ mask) for i in range(count)])


def place_of(diff, rounds):
    order = order_of(rounds)
    place = jnp.int32(0)
    for bit in [b for bits in rounds for b in bits]:
        step = order.index(bit)
        place = place + ((diff // bit) % 2) * step
    return place


def forward_kernel(rounds, blocks_ref, weeks_ref, mine_ref, other_ref, print_ref, out_ref, flux_ref):
    me = lax.axis_index("obs")
    half = mine_ref.shape[0]
    flux_ref[:half] = mine_ref[...]
    flux_ref[half:] = other_ref[...]
    slots, per_tile = print_ref.shape[:2]
    for tile in range(slots):
        total = None
        for j in range(0, per_tile, 2):
            first = place_of(blocks_ref[tile, j] ^ me, rounds)
            second = place_of(blocks_ref[tile, j + 1] ^ me, rounds)
            rows = jnp.concatenate([flux_ref[first], flux_ref[second]], axis=1)
            sens = jnp.concatenate([print_ref[tile, j], print_ref[tile, j + 1]], axis=1)
            part = lax.dot_general(
                rows, sens, (((1,), (1,)), ((), ())), preferred_element_type=jnp.float32
            )
            total = part if total is None else total + part
        weeks = weeks_ref[pl.ds(tile, 1), :]
        picked = total[:MEMBERS]
        for week in range(1, WEEKS):
            picked = jnp.where(weeks == week, total[week * MEMBERS : (week + 1) * MEMBERS], picked)
        out_ref[tile] = picked


def adjoint_kernel(
    rounds,
    blocks_ref,
    count_ref,
    ids_ref,
    weeks_ref,
    own_ref,
    far_ref,
    seen_ref,
    noise_ref,
    weight_ref,
    print_ref,
    keep_ref,
    send_ref,
    residual_ref,
    grad_ref,
):
    me = lax.axis_index("obs")
    slots, per_tile = print_ref.shape[:2]
    grad_ref[...] = jnp.zeros_like(grad_ref)
    count = count_ref[0]
    member = lax.broadcasted_iota(jnp.int32, (MEMBERS, MEMBERS), 1)
    row = lax.broadcasted_iota(jnp.int32, (MEMBERS, MEMBERS), 0)
    chosen = jnp.zeros((MEMBERS, MEMBERS), jnp.int32)
    for m in range(MEMBERS):
        chosen = jnp.where(row == m, ids_ref[m], chosen)
    hot = (member == chosen).astype(jnp.float32).astype(jnp.bfloat16)
    for tile in range(slots):
        shifted = jnp.dot(hot, noise_ref[tile], preferred_element_type=jnp.float32)
        alive = jnp.where(tile < count, jnp.float32(1), jnp.float32(0))
        weights = alive * weight_ref[pl.ds(tile, 1), :]
        seen = seen_ref[pl.ds(tile, 1), :]
        modeled = own_ref[tile] + far_ref[tile]
        residual = weights * (modeled - seen - shifted)
        residual_ref[tile] = residual.astype(jnp.bfloat16)
        weeks = weeks_ref[pl.ds(tile, 1), :]
        rows = jnp.concatenate(
            [jnp.where(weeks == week, residual, 0.0) for week in range(WEEKS)], axis=0
        ).astype(jnp.bfloat16)
        for j in range(0, per_tile, 2):
            first = place_of(blocks_ref[tile, j] ^ me, rounds)
            second = place_of(blocks_ref[tile, j + 1] ^ me, rounds)
            sens = jnp.concatenate([print_ref[tile, j], print_ref[tile, j + 1]], axis=1)
            part = jnp.dot(rows, sens, preferred_element_type=jnp.float32)
            cells = part.shape[1] // 2
            grad_ref[first] += part[:, :cells]
            grad_ref[second] += part[:, cells:]
    half = keep_ref.shape[0]
    keep_ref[...] = grad_ref[:half]
    send_ref[...] = grad_ref[half:]


def on_device(
    devices,
    slabs,
    flux_field,
    footprint,
    block_index,
    tile_count,
    sounding_week,
    member_ids,
    observed,
    perturb,
    obs_weight,
):
    rounds = phases_of(devices)
    slots, per_tile, sounds, cells = footprint.shape
    half = devices // 2
    params = pltpu.CompilerParams(vmem_limit_bytes=24 << 20)

    have = flux_field[0]
    for bits in rounds[:-1]:
        have = jnp.concatenate([have] + [swap(have, "obs", devices, m) for m in masks_of(bits)[1:]], axis=0)
    other = swap(have, "obs", devices, rounds[-1][0])
    modeled = pl.pallas_call(
        functools.partial(forward_kernel, rounds),
        out_shape=jax.ShapeDtypeStruct((slots, MEMBERS, sounds), jnp.float32),
        in_specs=[SMEM, VMEM, VMEM, VMEM, VMEM],
        out_specs=VMEM,
        scratch_shapes=[pltpu.VMEM((devices, ROWS, cells), jnp.bfloat16)],
        compiler_params=params,
        name="forward",
    )(block_index, sounding_week, have, other, footprint)
    mask = 1
    while 2 * mask < slabs:
        modeled = modeled + swap(modeled, "cell", slabs, mask)
        mask *= 2
    far = swap(modeled, "cell", slabs, mask)
    keep, send, residual = pl.pallas_call(
        functools.partial(adjoint_kernel, rounds),
        out_shape=(
            jax.ShapeDtypeStruct((half, ROWS, cells), jnp.float32),
            jax.ShapeDtypeStruct((half, ROWS, cells), jnp.float32),
            jax.ShapeDtypeStruct((slots, MEMBERS, sounds), jnp.bfloat16),
        ),
        in_specs=[SMEM, SMEM, SMEM] + [VMEM] * 7,
        out_specs=(VMEM, VMEM, VMEM),
        scratch_shapes=[pltpu.VMEM((devices, ROWS, cells), jnp.float32)],
        compiler_params=params,
        name="adjoint",
    )(
        block_index,
        tile_count,
        member_ids,
        sounding_week,
        modeled,
        far,
        observed,
        perturb,
        obs_weight,
        footprint,
    )
    total = keep + swap(send, "obs", devices, rounds[-1][0])
    for bits in rounds[-2::-1]:
        masks = masks_of(bits)
        pieces = jnp.split(total, len(masks), axis=0)
        total = pieces[0]
        for mask, piece in zip(masks[1:], pieces[1:]):
            total = total + swap(piece, "obs", devices, mask)
    return (total[None], residual)


def solution(mesh):
    devices, slabs = mesh.shape["obs"], mesh.shape["cell"]
    return jax.shard_map(
        functools.partial(on_device, devices, slabs),
        mesh=mesh,
        in_specs=(
            P("cell", "obs", None, None),
            P("obs", "cell", None, None),
            P("obs", "cell"),
            P("obs"),
            P("obs", None),
            P(),
            P("obs", None),
            P("obs", None, None),
            P("obs", None),
        ),
        out_specs=(P("cell", "obs", None, None), P("obs", None, None)),
        check_vma=False,
    )
```

```python
import functools

import jax
import jax.numpy as jnp
from jax import lax
from jax.experimental import pallas as pl
from jax.experimental.pallas import tpu as pltpu
from jax.sharding import PartitionSpec as P

MEMBERS = 16
WEEKS = 4
ROWS = WEEKS * MEMBERS

VMEM = pl.BlockSpec(memory_space=pltpu.VMEM)
SMEM = pl.BlockSpec(memory_space=pltpu.SMEM)
HBM = pl.BlockSpec(memory_space=pltpu.HBM)


def phases_of(count):
    bits = [1 << i for i in range(count.bit_length() - 1)]
    upper = bits[:0:-1]
    head = len(upper) % 2
    rounds = [upper[:1]] if head else []
    rounds += [upper[i : i + 2] for i in range(head, len(upper), 2)]
    return [sorted((m | 1 for m in masks_of(bits_of)[1:]), reverse=True) for bits_of in rounds]


def masks_of(bits):
    masks = [0]
    for bit in bits:
        masks += [mask | bit for mask in masks]
    return masks


def order_of(rounds):
    order = [0]
    for masks in rounds:
        order = [mask ^ low for mask in [0] + masks for low in order]
    return order


def swap(value, axis, count, mask):
    return lax.ppermute(value, axis, [(i, i ^ mask) for i in range(count)])


def prepare_kernel(
    rounds,
    gate_ref,
    count_ref,
    blocks_hbm,
    ids_hbm,
    weeks_hbm,
    seen_hbm,
    noise_hbm,
    weight_hbm,
    print_hbm,
    place_ref,
    weeks_ref,
    shift_ref,
    scale_ref,
    held_ref,
    blocks_ref,
    ids_ref,
    seen_ref,
    noise_ref,
    weight_ref,
    sems,
):
    pairs = (
        (blocks_hbm, blocks_ref),
        (ids_hbm, ids_ref),
        (noise_hbm, noise_ref),
        (seen_hbm, seen_ref),
        (weight_hbm, weight_ref),
        (weeks_hbm, weeks_ref),
        (print_hbm, held_ref),
    )
    copies = [pltpu.make_async_copy(src, dst, sems.at[i]) for i, (src, dst) in enumerate(pairs)]
    for copy in copies:
        copy.start()
    for copy in copies[:-1]:
        copy.wait()
    order = order_of(rounds)
    diff = blocks_ref[...] ^ lax.axis_index("obs")
    odd = diff & 1
    place = jnp.zeros_like(diff)
    for masks in rounds:
        low = diff & (functools.reduce(lambda a, b: a | b, masks) & ~1)
        for mask in masks:
            place = place + jnp.where(low == mask & ~1, order.index(mask), 0)
        odd = odd ^ jnp.where(low != 0, 1, 0)
    place_ref[...] = place + odd * len(order)
    column = lax.broadcasted_iota(jnp.int32, (MEMBERS, MEMBERS), 1)
    row = lax.broadcasted_iota(jnp.int32, (MEMBERS, MEMBERS), 0)
    chosen = jnp.zeros((MEMBERS, MEMBERS), jnp.int32)
    for m in range(MEMBERS):
        chosen = jnp.where(row == m, ids_ref[0, m], chosen)
    hot = (column == chosen).astype(jnp.float32).astype(jnp.bfloat16)
    for tile in range(shift_ref.shape[0]):
        shifted = jnp.dot(hot, noise_ref[tile], preferred_element_type=jnp.float32)
        shift_ref[tile] = seen_ref[pl.ds(tile, 1), :] + shifted
    alive = lax.broadcasted_iota(jnp.int32, weight_ref.shape, 0) < count_ref[0]
    scale_ref[...] = jnp.where(alive, jnp.float32(1), jnp.float32(0)) * weight_ref[...]
    copies[-1].wait()


def forward_kernel(place_ref, weeks_ref, mine_ref, other_ref, print_ref, out_ref, flux_ref):
    half = mine_ref.shape[0]
    flux_ref[:half] = mine_ref[...]
    flux_ref[half:] = other_ref[...]
    slots, per_tile = print_ref.shape[:2]
    for tile in range(slots):
        rows = jnp.concatenate([flux_ref[place_ref[j, tile]] for j in range(per_tile)], axis=1)
        sens = jnp.concatenate([print_ref[tile, j] for j in range(per_tile)], axis=1)
        total = lax.dot_general(
            rows, sens, (((1,), (1,)), ((), ())), preferred_element_type=jnp.float32
        )
        weeks = weeks_ref[pl.ds(tile, 1), :]
        picked = total[:MEMBERS]
        for week in range(1, WEEKS):
            picked = jnp.where(weeks == week, total[week * MEMBERS : (week + 1) * MEMBERS], picked)
        out_ref[tile] = picked


def adjoint_kernel(
    place_ref,
    weeks_ref,
    own_ref,
    far_ref,
    shift_ref,
    scale_ref,
    print_ref,
    keep_ref,
    send_ref,
    residual_ref,
    first_ref,
    second_ref,
):
    slots, per_tile = print_ref.shape[:2]
    sums = (first_ref, second_ref)
    for total_ref in sums:
        total_ref[...] = jnp.zeros_like(total_ref)
    for tile in range(slots):
        modeled = own_ref[tile] + far_ref[tile]
        residual = scale_ref[pl.ds(tile, 1), :] * (modeled - shift_ref[tile])
        residual_ref[tile] = residual
        weeks = weeks_ref[pl.ds(tile, 1), :]
        rows = jnp.concatenate(
            [jnp.where(weeks == week, residual, 0.0) for week in range(WEEKS)], axis=0
        ).astype(jnp.bfloat16)
        sens = jnp.concatenate([print_ref[tile, j] for j in range(per_tile)], axis=1)
        part = jnp.dot(rows, sens, preferred_element_type=jnp.float32)
        cells = part.shape[1] // per_tile
        for j in range(per_tile):
            sums[j % 2][place_ref[j, tile]] += part[:, j * cells : (j + 1) * cells]
    half = keep_ref.shape[0]
    keep_ref[...] = first_ref[:half] + second_ref[:half]
    send_ref[...] = first_ref[half:] + second_ref[half:]


def on_device(
    devices,
    slabs,
    flux_field,
    footprint,
    block_index,
    tile_count,
    sounding_week,
    member_ids,
    observed,
    perturb,
    obs_weight,
):
    rounds = phases_of(devices)
    slots, per_tile, sounds, cells = footprint.shape
    half = devices // 2
    params = pltpu.CompilerParams(vmem_limit_bytes=24 << 20)

    def shape(dims, kind):
        return jax.ShapeDtypeStruct(dims, kind)

    have = flux_field[0]
    for masks in rounds:
        gate = have
        got = [swap(have, "obs", devices, m) for m in masks[::-1]][::-1]
        if masks is rounds[-1]:
            break
        wide = lax.optimization_barrier(jnp.concatenate([have] * (len(masks) + 1), axis=0))
        for k, part in enumerate(got):
            wide = lax.dynamic_update_slice(wide, part, ((k + 1) * part.shape[0], 0, 0))
        have = wide
    parts = [have] + got
    small = (
        (block_index.T, pltpu.VMEM),
        (member_ids[None], pltpu.SMEM),
        (sounding_week, None),
        (observed, pltpu.VMEM),
        (perturb, pltpu.VMEM),
        (obs_weight, pltpu.VMEM),
    )
    place, weeks, shift, scale, held = pl.pallas_call(
        functools.partial(prepare_kernel, rounds),
        out_shape=(
            shape((per_tile, slots), jnp.int32),
            shape(sounding_week.shape, jnp.int32),
            shape((slots, MEMBERS, sounds), jnp.float32),
            shape((slots, sounds), jnp.float32),
            shape(footprint.shape, footprint.dtype),
        ),
        in_specs=[VMEM, SMEM] + [HBM] * 7,
        out_specs=(VMEM,) * 5,
        scratch_shapes=[kind(x.shape, x.dtype) for x, kind in small if kind]
        + [pltpu.SemaphoreType.DMA((7,))],
        compiler_params=params,
        cost_estimate=pl.CostEstimate(flops=0, bytes_accessed=2 * footprint.size * 2, transcendentals=0),
        name="prepare",
    )(
        gate,
        tile_count,
        *[pltpu.with_memory_space_constraint(x, pltpu.HBM) for x, _ in small],
        pltpu.with_memory_space_constraint(footprint, pltpu.HBM),
    )
    parts, shift = lax.optimization_barrier((parts, shift))
    have = jnp.concatenate(parts, axis=0)
    other = swap(have, "obs", devices, 1)
    modeled = pl.pallas_call(
        forward_kernel,
        out_shape=shape((slots, MEMBERS, sounds), jnp.float32),
        in_specs=[SMEM, VMEM, VMEM, VMEM, VMEM],
        out_specs=VMEM,
        scratch_shapes=[pltpu.VMEM((devices, ROWS, cells), jnp.bfloat16)],
        compiler_params=params,
        name="forward",
    )(place, weeks, have, other, held)
    mask = 1
    while 2 * mask < slabs:
        modeled = modeled + swap(modeled, "cell", slabs, mask)
        mask *= 2
    far = swap(modeled, "cell", slabs, mask)
    keep, send, residual = pl.pallas_call(
        adjoint_kernel,
        out_shape=(
            shape((half, ROWS, cells), jnp.float32),
            shape((half, ROWS, cells), jnp.float32),
            shape((slots, MEMBERS, sounds), jnp.float32),
        ),
        in_specs=[SMEM] + [VMEM] * 6,
        out_specs=(VMEM, VMEM, VMEM),
        scratch_shapes=[pltpu.VMEM((devices, ROWS, cells), jnp.float32)] * 2,
        compiler_params=params,
        name="adjoint",
    )(place, weeks, modeled, far, shift, scale, held)
    total = keep + swap(send, "obs", devices, 1)
    for masks in rounds[::-1]:
        pieces = jnp.split(total, len(masks) + 1, axis=0)
        total = pieces[0]
        for mask, piece in zip(masks, pieces[1:]):
            total = total + swap(piece, "obs", devices, mask)
    return (total[None], residual.astype(jnp.bfloat16))


def solution(mesh):
    devices, slabs = mesh.shape["obs"], mesh.shape["cell"]
    return jax.shard_map(
        functools.partial(on_device, devices, slabs),
        mesh=mesh,
        in_specs=(
            P("cell", "obs", None, None),
            P("obs", "cell", None, None),
            P("obs", "cell"),
            P("obs"),
            P("obs", None),
            P(),
            P("obs", None),
            P("obs", None, None),
            P("obs", None),
        ),
        out_specs=(P("cell", "obs", None, None), P("obs", None, None)),
        check_vma=False,
    )
```

```python
import functools

import jax
import jax.numpy as jnp
from jax import lax
from jax.experimental import pallas as pl
from jax.experimental.pallas import tpu as pltpu
from jax.sharding import PartitionSpec as P

MEMBERS = 16
WEEKS = 4
ROWS = WEEKS * MEMBERS

VMEM = pl.BlockSpec(memory_space=pltpu.VMEM)
SMEM = pl.BlockSpec(memory_space=pltpu.SMEM)
HBM = pl.BlockSpec(memory_space=pltpu.HBM)


def phases_of(count):
    bits = [1 << i for i in range(count.bit_length() - 1)]
    upper = bits[:0:-1]
    head = len(upper) % 2
    rounds = [upper[:1]] if head else []
    rounds += [upper[i : i + 2] for i in range(head, len(upper), 2)]
    return [sorted((m | 1 for m in masks_of(bits_of)[1:]), reverse=True) for bits_of in rounds]


def masks_of(bits):
    masks = [0]
    for bit in bits:
        masks += [mask | bit for mask in masks]
    return masks


def order_of(rounds):
    order = [0]
    for masks in rounds:
        order = [mask ^ low for mask in [0] + masks for low in order]
    return order


def swap(value, axis, count, mask):
    return lax.ppermute(value, axis, [(i, i ^ mask) for i in range(count)])


def prepare_kernel(
    rounds,
    gate_ref,
    count_ref,
    blocks_hbm,
    ids_hbm,
    weeks_hbm,
    seen_hbm,
    noise_hbm,
    weight_hbm,
    print_hbm,
    place_ref,
    weeks_ref,
    shift_ref,
    scale_ref,
    held_ref,
    blocks_ref,
    ids_ref,
    seen_ref,
    noise_ref,
    weight_ref,
    sems,
):
    pairs = (
        (blocks_hbm, blocks_ref),
        (ids_hbm, ids_ref),
        (noise_hbm, noise_ref),
        (seen_hbm, seen_ref),
        (weight_hbm, weight_ref),
        (weeks_hbm, weeks_ref),
        (print_hbm, held_ref),
    )
    copies = [pltpu.make_async_copy(src, dst, sems.at[i]) for i, (src, dst) in enumerate(pairs)]
    for copy in copies:
        copy.start()
    for copy in copies[:-1]:
        copy.wait()
    order = order_of(rounds)
    diff = blocks_ref[...] ^ lax.axis_index("obs")
    odd = diff & 1
    place = jnp.zeros_like(diff)
    for masks in rounds:
        low = diff & (functools.reduce(lambda a, b: a | b, masks) & ~1)
        for mask in masks:
            place = place + jnp.where(low == mask & ~1, order.index(mask), 0)
        odd = odd ^ jnp.where(low != 0, 1, 0)
    place_ref[...] = place + odd * len(order)
    column = lax.broadcasted_iota(jnp.int32, (MEMBERS, MEMBERS), 1)
    row = lax.broadcasted_iota(jnp.int32, (MEMBERS, MEMBERS), 0)
    chosen = jnp.zeros((MEMBERS, MEMBERS), jnp.int32)
    for m in range(MEMBERS):
        chosen = jnp.where(row == m, ids_ref[0, m], chosen)
    hot = (column == chosen).astype(jnp.float32).astype(jnp.bfloat16)
    for tile in range(shift_ref.shape[0]):
        shifted = jnp.dot(hot, noise_ref[tile], preferred_element_type=jnp.float32)
        shift_ref[tile] = seen_ref[pl.ds(tile, 1), :] + shifted
    alive = lax.broadcasted_iota(jnp.int32, weight_ref.shape, 0) < count_ref[0]
    scale_ref[...] = jnp.where(alive, jnp.float32(1), jnp.float32(0)) * weight_ref[...]
    copies[-1].wait()


def forward_kernel(place_ref, weeks_ref, mine_ref, other_ref, print_ref, out_ref, flux_ref):
    half = mine_ref.shape[0]
    flux_ref[:half] = mine_ref[...]
    flux_ref[half:] = other_ref[...]
    slots, per_tile = print_ref.shape[:2]
    for tile in range(slots):
        rows = jnp.concatenate([flux_ref[place_ref[j, tile]] for j in range(per_tile)], axis=1)
        sens = jnp.concatenate([print_ref[tile, j] for j in range(per_tile)], axis=1)
        total = lax.dot_general(
            rows, sens, (((1,), (1,)), ((), ())), preferred_element_type=jnp.float32
        )
        weeks = weeks_ref[pl.ds(tile, 1), :]
        picked = total[:MEMBERS]
        for week in range(1, WEEKS):
            picked = jnp.where(weeks == week, total[week * MEMBERS : (week + 1) * MEMBERS], picked)
        out_ref[tile] = picked


def adjoint_kernel(
    place_ref,
    weeks_ref,
    modeled_ref,
    shift_ref,
    scale_ref,
    print_ref,
    keep_ref,
    send_ref,
    residual_ref,
    first_ref,
    second_ref,
):
    slots, per_tile = print_ref.shape[:2]
    sums = (first_ref, second_ref)
    for total_ref in sums:
        total_ref[...] = jnp.zeros_like(total_ref)
    for tile in range(slots):
        residual = scale_ref[pl.ds(tile, 1), :] * (modeled_ref[tile] - shift_ref[tile])
        residual_ref[tile] = residual
        weeks = weeks_ref[pl.ds(tile, 1), :]
        rows = jnp.concatenate(
            [jnp.where(weeks == week, residual, 0.0) for week in range(WEEKS)], axis=0
        ).astype(jnp.bfloat16)
        sens = jnp.concatenate([print_ref[tile, j] for j in range(per_tile)], axis=1)
        part = jnp.dot(rows, sens, preferred_element_type=jnp.float32)
        cells = part.shape[1] // per_tile
        for j in range(per_tile):
            sums[j % 2][place_ref[j, tile]] += part[:, j * cells : (j + 1) * cells]
    half = keep_ref.shape[0]
    keep_ref[...] = first_ref[:half] + second_ref[:half]
    send_ref[...] = first_ref[half:] + second_ref[half:]


def on_device(
    devices,
    slabs,
    flux_field,
    footprint,
    block_index,
    tile_count,
    sounding_week,
    member_ids,
    observed,
    perturb,
    obs_weight,
):
    rounds = phases_of(devices)
    slots, per_tile, sounds, cells = footprint.shape
    half = devices // 2
    params = pltpu.CompilerParams(vmem_limit_bytes=24 << 20)

    def shape(dims, kind):
        return jax.ShapeDtypeStruct(dims, kind)

    have = flux_field[0]
    for masks in rounds:
        gate = have
        got = [swap(have, "obs", devices, m) for m in masks[::-1]][::-1]
        if masks is rounds[-1]:
            break
        wide = lax.optimization_barrier(jnp.concatenate([have] * (len(masks) + 1), axis=0))
        for k, part in enumerate(got):
            wide = lax.dynamic_update_slice(wide, part, ((k + 1) * part.shape[0], 0, 0))
        have = wide
    parts = [have] + got
    small = (
        (block_index.T, pltpu.VMEM),
        (member_ids[None], pltpu.SMEM),
        (sounding_week, None),
        (observed, pltpu.VMEM),
        (perturb, pltpu.VMEM),
        (obs_weight, pltpu.VMEM),
    )
    place, weeks, shift, scale, held = pl.pallas_call(
        functools.partial(prepare_kernel, rounds),
        out_shape=(
            shape((per_tile, slots), jnp.int32),
            shape(sounding_week.shape, jnp.int32),
            shape((slots, MEMBERS, sounds), jnp.float32),
            shape((slots, sounds), jnp.float32),
            shape(footprint.shape, footprint.dtype),
        ),
        in_specs=[VMEM, SMEM] + [HBM] * 7,
        out_specs=(VMEM,) * 5,
        scratch_shapes=[kind(x.shape, x.dtype) for x, kind in small if kind]
        + [pltpu.SemaphoreType.DMA((7,))],
        compiler_params=params,
        cost_estimate=pl.CostEstimate(flops=0, bytes_accessed=2 * footprint.size * 2, transcendentals=0),
        name="prepare",
    )(
        gate,
        tile_count,
        *[pltpu.with_memory_space_constraint(x, pltpu.HBM) for x, _ in small],
        pltpu.with_memory_space_constraint(footprint, pltpu.HBM),
    )
    parts, shift = lax.optimization_barrier((parts, shift))
    have = jnp.concatenate(parts, axis=0)
    other = swap(have, "obs", devices, 1)
    modeled = pl.pallas_call(
        forward_kernel,
        out_shape=shape((slots, MEMBERS, sounds), jnp.float32),
        in_specs=[SMEM, VMEM, VMEM, VMEM, VMEM],
        out_specs=VMEM,
        scratch_shapes=[pltpu.VMEM((devices, ROWS, cells), jnp.bfloat16)],
        compiler_params=params,
        name="forward",
    )(place, weeks, have, other, held)
    mask = 1
    while 2 * mask < slabs:
        modeled = modeled + swap(modeled, "cell", slabs, mask)
        mask *= 2
    modeled = modeled.astype(jnp.float16)
    far = swap(modeled, "cell", slabs, mask)
    modeled = modeled.astype(jnp.float32) + far.astype(jnp.float32)
    keep, send, residual = pl.pallas_call(
        adjoint_kernel,
        out_shape=(
            shape((half, ROWS, cells), jnp.float32),
            shape((half, ROWS, cells), jnp.float32),
            shape((slots, MEMBERS, sounds), jnp.float32),
        ),
        in_specs=[SMEM] + [VMEM] * 5,
        out_specs=(VMEM, VMEM, VMEM),
        scratch_shapes=[pltpu.VMEM((devices, ROWS, cells), jnp.float32)] * 2,
        compiler_params=params,
        name="adjoint",
    )(place, weeks, modeled, shift, scale, held)
    total = keep + swap(send, "obs", devices, 1)
    for masks in rounds[::-1]:
        pieces = jnp.split(total, len(masks) + 1, axis=0)
        total = pieces[0]
        for mask, piece in zip(masks, pieces[1:]):
            total = total + swap(piece, "obs", devices, mask)
    return (total[None], residual.astype(jnp.bfloat16))


def solution(mesh):
    devices, slabs = mesh.shape["obs"], mesh.shape["cell"]
    return jax.shard_map(
        functools.partial(on_device, devices, slabs),
        mesh=mesh,
        in_specs=(
            P("cell", "obs", None, None),
            P("obs", "cell", None, None),
            P("obs", "cell"),
            P("obs"),
            P("obs", None),
            P(),
            P("obs", None),
            P("obs", None, None),
            P("obs", None),
        ),
        out_specs=(P("cell", "obs", None, None), P("obs", None, None)),
        check_vma=False,
    )
```

```python
import functools
import math

import jax
import jax.numpy as jnp
from jax import lax
from jax.experimental import pallas as pl
from jax.experimental.pallas import tpu as pltpu
from jax.sharding import PartitionSpec as P

MEMBERS = 16
WEEKS = 4
ROWS = WEEKS * MEMBERS

VMEM = pl.BlockSpec(memory_space=pltpu.VMEM)
SMEM = pl.BlockSpec(memory_space=pltpu.SMEM)
HBM = pl.BlockSpec(memory_space=pltpu.HBM)


def phases_of(count):
    bits = [1 << i for i in range(count.bit_length() - 1)]
    upper = bits[:0:-1]
    head = len(upper) % 2
    rounds = [upper[:1]] if head else []
    rounds += [upper[i : i + 2] for i in range(head, len(upper), 2)]
    return [sorted((m | 1 for m in masks_of(bits_of)[1:]), reverse=True) for bits_of in rounds]


def masks_of(bits):
    masks = [0]
    for bit in bits:
        masks += [mask | bit for mask in masks]
    return masks


def order_of(rounds):
    order = [0]
    for masks in rounds:
        order = [mask ^ low for mask in [0] + masks for low in order]
    return order


def swap(value, axis, count, mask):
    return lax.ppermute(value, axis, [(i, i ^ mask) for i in range(count)])


def prepare_kernel(
    rounds,
    gate_ref,
    count_ref,
    blocks_hbm,
    ids_hbm,
    weeks_hbm,
    seen_hbm,
    noise_hbm,
    weight_hbm,
    print_hbm,
    place_ref,
    weeks_ref,
    shift_ref,
    scale_ref,
    held_ref,
    blocks_ref,
    ids_ref,
    seen_ref,
    noise_ref,
    weight_ref,
    sems,
):
    pairs = (
        (blocks_hbm, blocks_ref),
        (ids_hbm, ids_ref),
        (noise_hbm, noise_ref),
        (seen_hbm, seen_ref),
        (weight_hbm, weight_ref),
        (weeks_hbm, weeks_ref),
        (print_hbm, held_ref),
    )
    copies = [pltpu.make_async_copy(src, dst, sems.at[i]) for i, (src, dst) in enumerate(pairs)]
    for copy in copies:
        copy.start()
    for copy in copies[:-1]:
        copy.wait()
    order = order_of(rounds)
    diff = blocks_ref[...] ^ lax.axis_index("obs")
    odd = diff & 1
    place = jnp.zeros_like(diff)
    for masks in rounds:
        low = diff & (functools.reduce(lambda a, b: a | b, masks) & ~1)
        for mask in masks:
            place = place + jnp.where(low == mask & ~1, order.index(mask), 0)
        odd = odd ^ jnp.where(low != 0, 1, 0)
    place_ref[...] = place + odd * len(order)
    column = lax.broadcasted_iota(jnp.int32, (MEMBERS, MEMBERS), 1)
    row = lax.broadcasted_iota(jnp.int32, (MEMBERS, MEMBERS), 0)
    chosen = jnp.zeros((MEMBERS, MEMBERS), jnp.int32)
    for m in range(MEMBERS):
        chosen = jnp.where(row == m, ids_ref[0, m], chosen)
    hot = (column == chosen).astype(jnp.float32).astype(jnp.bfloat16)
    for tile in range(shift_ref.shape[0]):
        shifted = jnp.dot(hot, noise_ref[tile], preferred_element_type=jnp.float32)
        shift_ref[tile] = seen_ref[pl.ds(tile, 1), :] + shifted
    alive = lax.broadcasted_iota(jnp.int32, weight_ref.shape, 0) < count_ref[0]
    scale_ref[...] = jnp.where(alive, jnp.float32(1), jnp.float32(0)) * weight_ref[...]
    copies[-1].wait()


def forward_kernel(place_ref, weeks_ref, mine_ref, other_ref, print_ref, out_ref, flux_ref):
    half = mine_ref.shape[0]
    flux_ref[:half] = mine_ref[...]
    flux_ref[half:] = other_ref[...]
    slots, per_tile = print_ref.shape[:2]
    for tile in range(slots):
        rows = jnp.concatenate([flux_ref[place_ref[j, tile]] for j in range(per_tile)], axis=1)
        sens = jnp.concatenate([print_ref[tile, j] for j in range(per_tile)], axis=1)
        total = lax.dot_general(
            sens, rows, (((1,), (1,)), ((), ())), preferred_element_type=jnp.float32
        ).T
        weeks = weeks_ref[pl.ds(tile, 1), :]
        picked = total[:MEMBERS]
        for week in range(1, WEEKS):
            picked = jnp.where(weeks == week, total[week * MEMBERS : (week + 1) * MEMBERS], picked)
        out_ref[tile] = picked


def adjoint_kernel(
    place_ref,
    weeks_ref,
    modeled_ref,
    shift_ref,
    scale_ref,
    print_ref,
    keep_ref,
    send_ref,
    residual_ref,
    first_ref,
    second_ref,
):
    slots, per_tile = print_ref.shape[:2]
    sums = (first_ref, second_ref)
    for total_ref in sums:
        total_ref[...] = jnp.zeros_like(total_ref)
    for tile in range(slots):
        residual = scale_ref[pl.ds(tile, 1), :] * (modeled_ref[tile] - shift_ref[tile])
        residual_ref[tile] = residual
        weeks = weeks_ref[pl.ds(tile, 1), :]
        rows = jnp.concatenate(
            [jnp.where(weeks == week, residual, 0.0) for week in range(WEEKS)], axis=0
        ).astype(jnp.bfloat16)
        sens = jnp.concatenate([print_ref[tile, j] for j in range(per_tile)], axis=1)
        part = jnp.dot(rows, sens, preferred_element_type=jnp.float32)
        cells = part.shape[1] // per_tile
        for j in range(per_tile):
            sums[j % 2][place_ref[j, tile]] += part[:, j * cells : (j + 1) * cells]
    half = keep_ref.shape[0]
    keep_ref[...] = first_ref[:half] + second_ref[:half]
    send_ref[...] = first_ref[half:] + second_ref[half:]


def on_device(
    devices,
    slabs,
    flux_field,
    footprint,
    block_index,
    tile_count,
    sounding_week,
    member_ids,
    observed,
    perturb,
    obs_weight,
):
    rounds = phases_of(devices)
    slots, per_tile, sounds, cells = footprint.shape
    half = devices // 2
    params = pltpu.CompilerParams(vmem_limit_bytes=24 << 20)

    def shape(dims, kind):
        return jax.ShapeDtypeStruct(dims, kind)

    have = flux_field[0]
    for masks in rounds:
        gate = have
        got = [swap(have, "obs", devices, m) for m in masks[::-1]][::-1]
        if masks is rounds[-1]:
            break
        wide = lax.optimization_barrier(jnp.concatenate([have] * (len(masks) + 1), axis=0))
        for k, part in enumerate(got):
            wide = lax.dynamic_update_slice(wide, part, ((k + 1) * part.shape[0], 0, 0))
        have = wide
    parts = [have] + got
    small = (
        (block_index.T, pltpu.VMEM),
        (member_ids[None], pltpu.SMEM),
        (sounding_week, None),
        (observed, pltpu.VMEM),
        (perturb, pltpu.VMEM),
        (obs_weight, pltpu.VMEM),
    )
    place, weeks, shift, scale, held = pl.pallas_call(
        functools.partial(prepare_kernel, rounds),
        out_shape=(
            shape((per_tile, slots), jnp.int32),
            shape(sounding_week.shape, jnp.int32),
            shape((slots, MEMBERS, sounds), jnp.float32),
            shape((slots, sounds), jnp.float32),
            shape(footprint.shape, footprint.dtype),
        ),
        in_specs=[VMEM, SMEM] + [HBM] * 7,
        out_specs=(VMEM,) * 5,
        scratch_shapes=[kind(x.shape, x.dtype) for x, kind in small if kind]
        + [pltpu.SemaphoreType.DMA((7,))],
        compiler_params=params,
        cost_estimate=pl.CostEstimate(flops=0, bytes_accessed=2 * footprint.size * 2, transcendentals=0),
        name="prepare",
    )(
        gate,
        tile_count,
        *[pltpu.with_memory_space_constraint(x, pltpu.HBM) for x, _ in small],
        pltpu.with_memory_space_constraint(footprint, pltpu.HBM),
    )
    parts, shift = lax.optimization_barrier((parts, shift))
    have = jnp.concatenate(parts, axis=0)
    other = swap(have, "obs", devices, 1)
    modeled = pl.pallas_call(
        forward_kernel,
        out_shape=shape((slots, MEMBERS, sounds), jnp.float32),
        in_specs=[SMEM, VMEM, VMEM, VMEM, VMEM],
        out_specs=VMEM,
        scratch_shapes=[pltpu.VMEM((devices, ROWS, cells), jnp.bfloat16)],
        compiler_params=params,
        name="forward",
    )(place, weeks, have, other, held)
    mask = 1
    while 2 * mask < slabs:
        modeled = modeled + swap(modeled, "cell", slabs, mask)
        mask *= 2
    modeled = modeled.astype(jnp.float16)
    far = swap(modeled, "cell", slabs, mask)
    modeled = modeled.astype(jnp.float32) + far.astype(jnp.float32)
    keep, send, residual = pl.pallas_call(
        adjoint_kernel,
        out_shape=(
            shape((half, ROWS, cells), jnp.float32),
            shape((half, ROWS, cells), jnp.float32),
            shape((slots, MEMBERS, sounds), jnp.float32),
        ),
        in_specs=[SMEM] + [VMEM] * 5,
        out_specs=(VMEM, VMEM, VMEM),
        scratch_shapes=[pltpu.VMEM((devices, ROWS, cells), jnp.float32)] * 2,
        compiler_params=params,
        name="adjoint",
    )(place, weeks, modeled, shift, scale, held)
    peak = slots * per_tile * sounds * 0.125 * 3.0 * 1548.0

    def swap_sum(value, added, mask):
        scale = 2.0 ** math.ceil(math.log2(peak * added / 65504.0))
        sent = (value * (1.0 / scale)).astype(jnp.float16)
        return swap(sent, "obs", devices, mask).astype(jnp.float32) * scale

    added = 1
    total = keep + swap_sum(send, added, 1)
    added *= 2
    for masks in rounds[::-1]:
        pieces = jnp.split(total, len(masks) + 1, axis=0)
        total = pieces[0]
        for mask, piece in zip(masks, pieces[1:]):
            total = total + swap_sum(piece, added, mask)
        added *= len(masks) + 1
    return (total[None], residual.astype(jnp.bfloat16))


def solution(mesh):
    devices, slabs = mesh.shape["obs"], mesh.shape["cell"]
    return jax.shard_map(
        functools.partial(on_device, devices, slabs),
        mesh=mesh,
        in_specs=(
            P("cell", "obs", None, None),
            P("obs", "cell", None, None),
            P("obs", "cell"),
            P("obs"),
            P("obs", None),
            P(),
            P("obs", None),
            P("obs", None, None),
            P("obs", None),
        ),
        out_specs=(P("cell", "obs", None, None), P("obs", None, None)),
        check_vma=False,
    )
```

```python
import functools
import math

import jax
import jax.numpy as jnp
from jax import lax
from jax.experimental import pallas as pl
from jax.experimental.pallas import tpu as pltpu
from jax.sharding import PartitionSpec as P

MEMBERS = 16
WEEKS = 4
ROWS = WEEKS * MEMBERS

VMEM = pl.BlockSpec(memory_space=pltpu.VMEM)
SMEM = pl.BlockSpec(memory_space=pltpu.SMEM)
HBM = pl.BlockSpec(memory_space=pltpu.HBM)


def phases_of(count):
    bits = [1 << i for i in range(count.bit_length() - 1)]
    upper = bits[:0:-1]
    head = len(upper) % 2
    rounds = [upper[:1]] if head else []
    rounds += [upper[i : i + 2] for i in range(head, len(upper), 2)]
    return [sorted((m | 1 for m in masks_of(bits_of)[1:]), reverse=True) for bits_of in rounds]


def masks_of(bits):
    masks = [0]
    for bit in bits:
        masks += [mask | bit for mask in masks]
    return masks


def order_of(rounds):
    order = [0]
    for masks in rounds:
        order = [mask ^ low for mask in [0] + masks for low in order]
    return order


def swap(value, axis, count, mask):
    return lax.ppermute(value, axis, [(i, i ^ mask) for i in range(count)])


def prepare_kernel(
    rounds,
    gate_ref,
    blocks_hbm,
    ids_hbm,
    weeks_hbm,
    seen_hbm,
    noise_hbm,
    weight_hbm,
    print_hbm,
    place_ref,
    weeks_ref,
    shift_ref,
    weight_ref,
    held_ref,
    blocks_ref,
    ids_ref,
    seen_ref,
    noise_ref,
    sems,
):
    pairs = (
        (blocks_hbm, blocks_ref),
        (ids_hbm, ids_ref),
        (noise_hbm, noise_ref),
        (seen_hbm, seen_ref),
        (weight_hbm, weight_ref),
        (weeks_hbm, weeks_ref),
        (print_hbm, held_ref),
    )
    copies = [pltpu.make_async_copy(src, dst, sems.at[i]) for i, (src, dst) in enumerate(pairs)]
    for copy in copies:
        copy.start()
    for copy in copies[:-1]:
        copy.wait()
    order = order_of(rounds)
    diff = blocks_ref[...] ^ lax.axis_index("obs")
    odd = diff & 1
    place = jnp.zeros_like(diff)
    for masks in rounds:
        low = diff & (functools.reduce(lambda a, b: a | b, masks) & ~1)
        for mask in masks:
            place = place + jnp.where(low == mask & ~1, order.index(mask), 0)
        odd = odd ^ jnp.where(low != 0, 1, 0)
    place_ref[...] = place + odd * len(order)
    column = lax.broadcasted_iota(jnp.int32, (MEMBERS, MEMBERS), 1)
    row = lax.broadcasted_iota(jnp.int32, (MEMBERS, MEMBERS), 0)
    chosen = jnp.zeros((MEMBERS, MEMBERS), jnp.int32)
    for m in range(MEMBERS):
        chosen = jnp.where(row == m, ids_ref[0, m], chosen)
    hot = (column == chosen).astype(jnp.float32).astype(jnp.bfloat16)
    for tile in range(shift_ref.shape[0]):
        shifted = jnp.dot(hot, noise_ref[tile], preferred_element_type=jnp.float32)
        shift_ref[tile] = seen_ref[pl.ds(tile, 1), :] + shifted
    copies[-1].wait()


def forward_kernel(place_ref, weeks_ref, mine_ref, other_ref, print_ref, out_ref, flux_ref):
    half = mine_ref.shape[0]
    flux_ref[:half] = mine_ref[...]
    flux_ref[half:] = other_ref[...]
    slots, per_tile = print_ref.shape[:2]
    for tile in range(slots):
        rows = jnp.concatenate([flux_ref[place_ref[j, tile]] for j in range(per_tile)], axis=1)
        sens = jnp.concatenate([print_ref[tile, j] for j in range(per_tile)], axis=1)
        total = lax.dot_general(
            sens, rows, (((1,), (1,)), ((), ())), preferred_element_type=jnp.float32
        ).T
        weeks = weeks_ref[pl.ds(tile, 1), :]
        picked = total[:MEMBERS]
        for week in range(1, WEEKS):
            picked = jnp.where(weeks == week, total[week * MEMBERS : (week + 1) * MEMBERS], picked)
        out_ref[tile] = picked


def adjoint_kernel(
    count_ref,
    place_ref,
    weeks_ref,
    modeled_ref,
    shift_ref,
    weight_ref,
    print_ref,
    keep_ref,
    send_ref,
    residual_ref,
    first_ref,
    second_ref,
):
    slots, per_tile = print_ref.shape[:2]
    sums = (first_ref, second_ref)
    count = count_ref[0]
    for total_ref in sums:
        total_ref[...] = jnp.zeros_like(total_ref)
    for tile in range(slots):
        alive = jnp.where(tile < count, jnp.float32(1), jnp.float32(0))
        residual = (alive * weight_ref[pl.ds(tile, 1), :]) * (modeled_ref[tile] - shift_ref[tile])
        residual_ref[tile] = residual
        weeks = weeks_ref[pl.ds(tile, 1), :]
        rows = jnp.concatenate(
            [jnp.where(weeks == week, residual, 0.0) for week in range(WEEKS)], axis=0
        ).astype(jnp.bfloat16)
        sens = jnp.concatenate([print_ref[tile, j] for j in range(per_tile)], axis=1)
        part = jnp.dot(rows, sens, preferred_element_type=jnp.float32)
        cells = part.shape[1] // per_tile
        for j in range(per_tile):
            sums[j % 2][place_ref[j, tile]] += part[:, j * cells : (j + 1) * cells]
    half = keep_ref.shape[0]
    keep_ref[...] = first_ref[:half] + second_ref[:half]
    send_ref[...] = first_ref[half:] + second_ref[half:]


def on_device(
    devices,
    slabs,
    flux_field,
    footprint,
    block_index,
    tile_count,
    sounding_week,
    member_ids,
    observed,
    perturb,
    obs_weight,
):
    rounds = phases_of(devices)
    slots, per_tile, sounds, cells = footprint.shape
    half = devices // 2
    params = pltpu.CompilerParams(vmem_limit_bytes=24 << 20)

    def shape(dims, kind):
        return jax.ShapeDtypeStruct(dims, kind)

    have = flux_field[0]
    for masks in rounds:
        gate = have
        got = [swap(have, "obs", devices, m) for m in masks[::-1]][::-1]
        if masks is rounds[-1]:
            break
        wide = lax.optimization_barrier(jnp.concatenate([have] * (len(masks) + 1), axis=0))
        for k, part in enumerate(got):
            wide = lax.dynamic_update_slice(wide, part, ((k + 1) * part.shape[0], 0, 0))
        have = wide
    parts = [have] + got
    small = (
        (block_index.T, pltpu.VMEM),
        (member_ids[None], pltpu.SMEM),
        (sounding_week, None),
        (observed, pltpu.VMEM),
        (perturb, pltpu.VMEM),
        (obs_weight, None),
    )
    place, weeks, shift, weight, held = pl.pallas_call(
        functools.partial(prepare_kernel, rounds),
        out_shape=(
            shape((per_tile, slots), jnp.int32),
            shape(sounding_week.shape, jnp.int32),
            shape((slots, MEMBERS, sounds), jnp.float32),
            shape((slots, sounds), jnp.float32),
            shape(footprint.shape, footprint.dtype),
        ),
        in_specs=[VMEM] + [HBM] * 7,
        out_specs=(VMEM,) * 5,
        scratch_shapes=[kind(x.shape, x.dtype) for x, kind in small if kind]
        + [pltpu.SemaphoreType.DMA((7,))],
        compiler_params=params,
        cost_estimate=pl.CostEstimate(flops=0, bytes_accessed=2 * footprint.size * 2, transcendentals=0),
        name="prepare",
    )(
        gate,
        *[pltpu.with_memory_space_constraint(x, pltpu.HBM) for x, _ in small],
        pltpu.with_memory_space_constraint(footprint, pltpu.HBM),
    )
    parts, shift = lax.optimization_barrier((parts, shift))
    have = jnp.concatenate(parts, axis=0)
    other = swap(have, "obs", devices, 1)
    modeled = pl.pallas_call(
        forward_kernel,
        out_shape=shape((slots, MEMBERS, sounds), jnp.float32),
        in_specs=[SMEM, VMEM, VMEM, VMEM, VMEM],
        out_specs=VMEM,
        scratch_shapes=[pltpu.VMEM((devices, ROWS, cells), jnp.bfloat16)],
        compiler_params=params,
        name="forward",
    )(place, weeks, have, other, held)
    mask = 1
    while 2 * mask < slabs:
        modeled = modeled + swap(modeled, "cell", slabs, mask)
        mask *= 2
    modeled = modeled.astype(jnp.float16)
    far = swap(modeled, "cell", slabs, mask)
    modeled = modeled.astype(jnp.float32) + far.astype(jnp.float32)
    keep, send, residual = pl.pallas_call(
        adjoint_kernel,
        out_shape=(
            shape((half, ROWS, cells), jnp.float32),
            shape((half, ROWS, cells), jnp.float32),
            shape((slots, MEMBERS, sounds), jnp.float32),
        ),
        in_specs=[SMEM, SMEM] + [VMEM] * 5,
        out_specs=(VMEM, VMEM, VMEM),
        scratch_shapes=[pltpu.VMEM((devices, ROWS, cells), jnp.float32)] * 2,
        compiler_params=params,
        name="adjoint",
    )(tile_count, place, weeks, modeled, shift, weight, held)
    peak = slots * per_tile * sounds * 0.125 * 3.0 * 1548.0

    def swap_sum(value, added, mask):
        scale = 2.0 ** math.ceil(math.log2(peak * added / 65504.0))
        sent = (value * (1.0 / scale)).astype(jnp.float16)
        return swap(sent, "obs", devices, mask).astype(jnp.float32) * scale

    added = 1
    total = keep + swap_sum(send, added, 1)
    added *= 2
    for masks in rounds[::-1]:
        pieces = jnp.split(total, len(masks) + 1, axis=0)
        total = pieces[0]
        for mask, piece in zip(masks, pieces[1:]):
            total = total + swap_sum(piece, added, mask)
        added *= len(masks) + 1
    return (total[None], residual.astype(jnp.bfloat16))


def solution(mesh):
    devices, slabs = mesh.shape["obs"], mesh.shape["cell"]
    return jax.shard_map(
        functools.partial(on_device, devices, slabs),
        mesh=mesh,
        in_specs=(
            P("cell", "obs", None, None),
            P("obs", "cell", None, None),
            P("obs", "cell"),
            P("obs"),
            P("obs", None),
            P(),
            P("obs", None),
            P("obs", None, None),
            P("obs", None),
        ),
        out_specs=(P("cell", "obs", None, None), P("obs", None, None)),
        check_vma=False,
    )
```

```python
import functools
import math

import jax
import jax.numpy as jnp
from jax import lax
from jax.experimental import pallas as pl
from jax.experimental.pallas import tpu as pltpu
from jax.sharding import PartitionSpec as P

MEMBERS = 16
WEEKS = 4
ROWS = WEEKS * MEMBERS

VMEM = pl.BlockSpec(memory_space=pltpu.VMEM)
SMEM = pl.BlockSpec(memory_space=pltpu.SMEM)
HBM = pl.BlockSpec(memory_space=pltpu.HBM)


def phases_of(count):
    bits = [1 << i for i in range(count.bit_length() - 1)]
    upper = bits[:0:-1]
    head = len(upper) % 2
    rounds = [upper[:1]] if head else []
    rounds += [upper[i : i + 2] for i in range(head, len(upper), 2)]
    return [sorted((m | 1 for m in masks_of(bits_of)[1:]), reverse=True) for bits_of in rounds]


def masks_of(bits):
    masks = [0]
    for bit in bits:
        masks += [mask | bit for mask in masks]
    return masks


def order_of(rounds):
    order = [0]
    for masks in rounds:
        order = [mask ^ low for mask in [0] + masks for low in order]
    return order


def swap(value, axis, count, mask):
    return lax.ppermute(value, axis, [(i, i ^ mask) for i in range(count)])


def prepare_kernel(
    rounds,
    gate_ref,
    blocks_hbm,
    ids_hbm,
    weeks_hbm,
    seen_hbm,
    noise_hbm,
    weight_hbm,
    print_hbm,
    place_ref,
    weeks_ref,
    shift_ref,
    weight_ref,
    held_ref,
    blocks_ref,
    ids_ref,
    seen_ref,
    noise_ref,
    table_ref,
    sems,
):
    pairs = (
        (blocks_hbm, blocks_ref),
        (ids_hbm, ids_ref),
        (noise_hbm, noise_ref),
        (seen_hbm, seen_ref),
        (weight_hbm, weight_ref),
        (weeks_hbm, weeks_ref),
        (print_hbm, held_ref),
    )
    copies = [pltpu.make_async_copy(src, dst, sems.at[i]) for i, (src, dst) in enumerate(pairs)]
    for copy in copies:
        copy.start()
    for copy in copies[:-1]:
        copy.wait()
    order = order_of(rounds)
    diff = blocks_ref[...] ^ lax.axis_index("obs")
    odd = diff & 1
    place = jnp.zeros_like(diff)
    for masks in rounds:
        low = diff & (functools.reduce(lambda a, b: a | b, masks) & ~1)
        for mask in masks:
            place = place + jnp.where(low == mask & ~1, order.index(mask), 0)
        odd = odd ^ jnp.where(low != 0, 1, 0)
    table_ref[...] = place + odd * len(order)
    spread = pltpu.make_async_copy(table_ref, place_ref, sems.at[len(pairs)])
    spread.start()
    column = lax.broadcasted_iota(jnp.int32, (MEMBERS, MEMBERS), 1)
    row = lax.broadcasted_iota(jnp.int32, (MEMBERS, MEMBERS), 0)
    chosen = jnp.zeros((MEMBERS, MEMBERS), jnp.int32)
    for m in range(MEMBERS):
        chosen = jnp.where(row == m, ids_ref[0, m], chosen)
    hot = (column == chosen).astype(jnp.float32).astype(jnp.bfloat16)
    for tile in range(shift_ref.shape[0]):
        shifted = jnp.dot(hot, noise_ref[tile], preferred_element_type=jnp.float32)
        shift_ref[tile] = seen_ref[pl.ds(tile, 1), :] + shifted
    spread.wait()
    copies[-1].wait()


def forward_kernel(place_ref, weeks_ref, mine_ref, other_ref, print_ref, out_ref, flux_ref):
    half = mine_ref.shape[0]
    flux_ref[:half] = mine_ref[...]
    flux_ref[half:] = other_ref[...]
    slots, per_tile = print_ref.shape[:2]
    for tile in range(slots):
        rows = jnp.concatenate([flux_ref[place_ref[j, tile]] for j in range(per_tile)], axis=1)
        sens = jnp.concatenate([print_ref[tile, j] for j in range(per_tile)], axis=1)
        total = lax.dot_general(
            sens, rows, (((1,), (1,)), ((), ())), preferred_element_type=jnp.float32
        ).T
        weeks = weeks_ref[pl.ds(tile, 1), :]
        picked = total[:MEMBERS]
        for week in range(1, WEEKS):
            picked = jnp.where(weeks == week, total[week * MEMBERS : (week + 1) * MEMBERS], picked)
        out_ref[tile] = picked


def adjoint_kernel(
    count_ref,
    place_ref,
    weeks_ref,
    modeled_ref,
    shift_ref,
    weight_ref,
    print_ref,
    keep_ref,
    send_ref,
    residual_ref,
    first_ref,
    second_ref,
):
    slots, per_tile = print_ref.shape[:2]
    sums = (first_ref, second_ref)
    count = count_ref[0]
    for total_ref in sums:
        total_ref[...] = jnp.zeros_like(total_ref)
    for tile in range(slots):
        alive = jnp.where(tile < count, jnp.float32(1), jnp.float32(0))
        residual = (alive * weight_ref[pl.ds(tile, 1), :]) * (modeled_ref[tile] - shift_ref[tile])
        residual_ref[tile] = residual
        weeks = weeks_ref[pl.ds(tile, 1), :]
        rows = jnp.concatenate(
            [jnp.where(weeks == week, residual, 0.0) for week in range(WEEKS)], axis=0
        ).astype(jnp.bfloat16)
        sens = jnp.concatenate([print_ref[tile, j] for j in range(per_tile)], axis=1)
        part = jnp.dot(rows, sens, preferred_element_type=jnp.float32)
        cells = part.shape[1] // per_tile
        for j in range(per_tile):
            sums[j % 2][place_ref[j, tile]] += part[:, j * cells : (j + 1) * cells]
    half = keep_ref.shape[0]
    keep_ref[...] = first_ref[:half] + second_ref[:half]
    send_ref[...] = first_ref[half:] + second_ref[half:]


def on_device(
    devices,
    slabs,
    flux_field,
    footprint,
    block_index,
    tile_count,
    sounding_week,
    member_ids,
    observed,
    perturb,
    obs_weight,
):
    rounds = phases_of(devices)
    slots, per_tile, sounds, cells = footprint.shape
    half = devices // 2
    params = pltpu.CompilerParams(vmem_limit_bytes=24 << 20)

    def shape(dims, kind):
        return jax.ShapeDtypeStruct(dims, kind)

    have = flux_field[0]
    for masks in rounds:
        gate = have
        got = [swap(have, "obs", devices, m) for m in masks[::-1]][::-1]
        if masks is rounds[-1]:
            break
        wide = lax.optimization_barrier(jnp.concatenate([have] * (len(masks) + 1), axis=0))
        for k, part in enumerate(got):
            wide = lax.dynamic_update_slice(wide, part, ((k + 1) * part.shape[0], 0, 0))
        have = wide
    parts = [have] + got
    small = (
        (block_index.T, pltpu.VMEM),
        (member_ids[None], pltpu.SMEM),
        (sounding_week, None),
        (observed, pltpu.VMEM),
        (perturb, pltpu.VMEM),
        (obs_weight, None),
    )
    place, weeks, shift, weight, held = pl.pallas_call(
        functools.partial(prepare_kernel, rounds),
        out_shape=(
            pltpu.SMEM((per_tile, slots), jnp.int32),
            shape(sounding_week.shape, jnp.int32),
            shape((slots, MEMBERS, sounds), jnp.float32),
            shape((slots, sounds), jnp.float32),
            shape(footprint.shape, footprint.dtype),
        ),
        in_specs=[VMEM] + [HBM] * 7,
        out_specs=(SMEM,) + (VMEM,) * 4,
        scratch_shapes=[kind(x.shape, x.dtype) for x, kind in small if kind]
        + [pltpu.VMEM((per_tile, slots), jnp.int32), pltpu.SemaphoreType.DMA((8,))],
        compiler_params=params,
        cost_estimate=pl.CostEstimate(flops=0, bytes_accessed=2 * footprint.size * 2, transcendentals=0),
        name="prepare",
    )(
        gate,
        *[pltpu.with_memory_space_constraint(x, pltpu.HBM) for x, _ in small],
        pltpu.with_memory_space_constraint(footprint, pltpu.HBM),
    )
    parts, shift = lax.optimization_barrier((parts, shift))
    have = jnp.concatenate(parts, axis=0)
    other = swap(have, "obs", devices, 1)
    modeled = pl.pallas_call(
        forward_kernel,
        out_shape=shape((slots, MEMBERS, sounds), jnp.float32),
        in_specs=[SMEM, VMEM, VMEM, VMEM, VMEM],
        out_specs=VMEM,
        scratch_shapes=[pltpu.VMEM((devices, ROWS, cells), jnp.bfloat16)],
        compiler_params=params,
        name="forward",
    )(place, weeks, have, other, held)
    mask = 1
    while 2 * mask < slabs:
        modeled = modeled + swap(modeled, "cell", slabs, mask)
        mask *= 2
    modeled = modeled.astype(jnp.float16)
    far = swap(modeled, "cell", slabs, mask)
    modeled = modeled.astype(jnp.float32) + far.astype(jnp.float32)
    keep, send, residual = pl.pallas_call(
        adjoint_kernel,
        out_shape=(
            shape((half, ROWS, cells), jnp.float32),
            shape((half, ROWS, cells), jnp.float32),
            shape((slots, MEMBERS, sounds), jnp.float32),
        ),
        in_specs=[SMEM, SMEM] + [VMEM] * 5,
        out_specs=(VMEM, VMEM, VMEM),
        scratch_shapes=[pltpu.VMEM((devices, ROWS, cells), jnp.float32)] * 2,
        compiler_params=params,
        name="adjoint",
    )(tile_count, place, weeks, modeled, shift, weight, held)
    peak = slots * per_tile * sounds * 0.125 * 3.0 * 1548.0

    def swap_sum(value, added, mask):
        scale = 2.0 ** math.ceil(math.log2(peak * added / 65504.0))
        sent = (value * (1.0 / scale)).astype(jnp.float16)
        return swap(sent, "obs", devices, mask).astype(jnp.float32) * scale

    added = 1
    total = keep + swap_sum(send, added, 1)
    added *= 2
    for masks in rounds[::-1]:
        pieces = jnp.split(total, len(masks) + 1, axis=0)
        total = pieces[0]
        for mask, piece in zip(masks, pieces[1:]):
            total = total + swap_sum(piece, added, mask)
        added *= len(masks) + 1
    return (total[None], residual.astype(jnp.bfloat16))


def solution(mesh):
    devices, slabs = mesh.shape["obs"], mesh.shape["cell"]
    return jax.shard_map(
        functools.partial(on_device, devices, slabs),
        mesh=mesh,
        in_specs=(
            P("cell", "obs", None, None),
            P("obs", "cell", None, None),
            P("obs", "cell"),
            P("obs"),
            P("obs", None),
            P(),
            P("obs", None),
            P("obs", None, None),
            P("obs", None),
        ),
        out_specs=(P("cell", "obs", None, None), P("obs", None, None)),
        check_vma=False,
    )
```
